32 devices in a mesh: row: 4 (over y, x), seq: 8 (over z, core).
Axes of the slice: x: 2, y: 2, z: 4, core: 2. Of those that a mesh axis runs over, the one named last changes fastest.
Arguments:
- hidden_in: bfloat16 [4, 1024, 2048], P('row', 'seq'), may hold values from -6 to 6
- positions: int32 [4, 1024], P('row', 'seq'), may hold values from 0 to 7164, as said below
- languages: int32 [4], replicated, may hold values from 0 to 6
- ln1_gain: bfloat16 [2048], replicated, may hold values from 0.5 to 1.5
- ln1_bias: bfloat16 [2048], replicated, may hold values from -1.1953125 to 1.1953125
- w_qkv: bfloat16 [2048, 6144], P(None, 'seq'), may hold values from -0.125 to 0.125
- b_qkv: bfloat16 [6144], P('seq'), may hold values from -1.1953125 to 1.1953125
- w_out: bfloat16 [2048, 2048], P('seq'), may hold values from -3 to 3
- ln2_gain: bfloat16 [2048], replicated, may hold values from 0.5 to 1.5
- ln2_bias: bfloat16 [2048], replicated, may hold values from -1.1953125 to 1.1953125
- w_gate: bfloat16 [2048, 5632], P(None, 'seq'), may hold values from -0.125 to 0.125
- w_up: bfloat16 [2048, 5632], P(None, 'seq'), may hold values from -0.125 to 0.125
- w_down: bfloat16 [5632, 2048], P('seq'), may hold values from -0.078125 to 0.078125
- cotangent: bfloat16 [4, 1024, 2048], P('row', 'seq'), may hold values from -6 to 6
Outputs:
- output: bfloat16 [4, 1024, 2048], P('row', 'seq')
- input_grad: bfloat16 [4, 1024, 2048], P('row', 'seq')
- grad_ln1_gain: float32 [2048], P('seq')
- grad_ln1_bias: float32 [2048], P('seq')
- grad_w_qkv: float32 [2048, 6144], P(None, 'seq')
- grad_b_qkv: float32 [6144], P('seq')
- grad_w_out: float32 [2048, 2048], P('seq')
- grad_ln2_gain: float32 [2048], P('seq')
- grad_ln2_bias: float32 [2048], P('seq')
- grad_w_gate: float32 [2048, 5632], P(None, 'seq')
- grad_w_up: float32 [2048, 5632], P(None, 'seq')
- grad_w_down: float32 [5632, 2048], P('seq')
The draws below stay inside these ranges and needn't reach their ends.
Inputs may be any that keep to these rules, and one draw needn't show every extreme that they name: Each sequence's positions start at an offset of 0 to 4095 and rise by 1 to 3 from one token to the next; some sequence starts at 0, and another starts at 4095 and rises by 3 at every token.
All inputs are finite; a program needn't handle non-finite values.
Results may differ from the reference program's by a relative error of at most 0.013.
Values may be sent and summed in bfloat16 or wider, within the bound.
No kernel may reach another device: no remote copies, remote signals or barrier semaphores. Data moves between devices by JAX's collectives and lax.ppermute only.
A program may use at most 256 MiB of HBM per device.

```python
import math
import jax
import jax.numpy as jnp
from jax import lax

D = 2048
HEADS = 32
HEAD_DIM = 64
FF = 5632
ROT = 16
LANGS = 7
ROWS = 4
LEN = 1024


def draw_positions(key, part):
    offset_key = jax.random.fold_in(key, 11)
    pick_key = jax.random.fold_in(key, 23)
    step_key = jax.random.fold_in(key, 37)
    offsets = jax.random.randint(offset_key, (ROWS, 1), 0, 4096)
    chosen = jax.random.randint(pick_key, (), 0, ROWS)
    row_ids = jnp.arange(ROWS)[:, None]
    offsets = jnp.where(row_ids == chosen, 4095, offsets)
    offsets = jnp.where(row_ids == (chosen + 1) % ROWS, 0, offsets)
    strides = jax.random.randint(step_key, (ROWS, LEN), 1, 4)
    strides = jnp.where(row_ids == chosen, 3, strides)
    col_ids = jnp.arange(LEN)[None, :]
    strides = jnp.where(col_ids == 0, 0, strides)
    return (offsets + jnp.cumsum(strides, axis=1)).astype(jnp.int32)


def with_ends(drawn, stream_key, smallest, top_value):
    longest = drawn.shape.index(max(drawn.shape))
    spots = []
    for shift in (0, 1):
        where = [jax.random.randint(jax.random.fold_in(stream_key, axis), (), 0, length) for axis, length in enumerate(drawn.shape)]
        where[longest] = (where[longest] + shift) % drawn.shape[longest]
        spots.append(tuple(where))
    return drawn.at[spots[0]].set(smallest).at[spots[1]].set(top_value)


def levels(rng, dims, shards, least, top_value):
    level, own = 1.0, jax.random.fold_in(rng, 6)
    for axis_at, shards_of in shards:
        draws = jnp.exp(jax.random.uniform(jax.random.fold_in(own, axis_at), (shards_of,), jnp.float32, least / len(shards), top_value / len(shards)))
        level = level * jnp.repeat(draws, dims[axis_at] // shards_of).reshape([-1 if axis == axis_at else 1 for axis in range(len(dims))])
    return level


def bell_draw(own_key, extent, scale, limit, shards=(), kind=jnp.bfloat16):
    values = jax.random.normal(own_key, extent, jnp.float32) * scale
    if len(shards) > 0:
        values = levels(own_key, extent, shards, -0.22, 0.18) * values
    return jnp.clip(values, min=-limit, max=limit).astype(kind)


def setup_inputs(seed: int = 0) -> dict:
    key_of = jax.random.split(jax.random.key(seed), 15)
    hidden_in = bell_draw(key_of[0], (ROWS, LEN, D), 1.0, 6.0, ((0, 4), (1, 8)))
    positions = draw_positions(jax.random.fold_in(key_of[14], 71), 0)
    languages = with_ends(jax.random.randint(key_of[2], (ROWS,), 0, LANGS), jax.random.fold_in(key_of[2], 1), 0, LANGS - 1).astype(jnp.int32)
    ln1_gain = jnp.clip(1.0 + 0.1 * jax.random.normal(key_of[3], (D,), jnp.float32), 0.5, 1.5).astype(jnp.bfloat16)
    ln1_bias = bell_draw(key_of[4], (D,), 0.2, 1.1953125)
    w_qkv = bell_draw(key_of[5], (D, 3 * D), D ** -0.5, 0.125, ((1, 8),))
    b_qkv = bell_draw(key_of[6], (3 * D,), 0.2, 1.1953125, ((0, 8),))
    w_out = bell_draw(key_of[7], (D, D), (max(D // 512, 1)) ** -0.5, 3.0, ((0, 8),))
    ln2_gain = jnp.clip(1.0 + 0.1 * jax.random.normal(key_of[8], (D,), jnp.float32), 0.5, 1.5).astype(jnp.bfloat16)
    ln2_bias = bell_draw(key_of[9], (D,), 0.2, 1.1953125)
    w_gate = bell_draw(key_of[10], (D, FF), D ** -0.5, 0.125, ((1, 8),))
    w_up = bell_draw(key_of[11], (D, FF), D ** -0.5, 0.125, ((1, 8),))
    w_down = bell_draw(key_of[12], (FF, D), FF ** -0.5, 0.078125, ((0, 8),))
    cotangent = bell_draw(key_of[13], (ROWS, LEN, D), 1.0, 6.0, ((0, 4), (1, 8)))
    return dict(hidden_in=hidden_in, positions=positions, languages=languages, ln1_gain=ln1_gain, ln1_bias=ln1_bias, w_qkv=w_qkv, b_qkv=b_qkv, w_out=w_out, ln2_gain=ln2_gain, ln2_bias=ln2_bias, w_gate=w_gate, w_up=w_up, w_down=w_down, cotangent=cotangent)


EPS = 1e-05
NEG = -1e+30
BASE = 10000.0

@jax.custom_vjp
def low(v):
    return lax.optimization_barrier(v.astype(jnp.bfloat16)).astype(jnp.float32)

@jax.custom_vjp
def low_back(v):
    return v

def low_keep(v):
    return (low(v), None)

def low_pass(kept, grad):
    return (grad,)

def back_keep(v):
    return (v, None)

def back_low(kept, grad):
    return (low(grad),)
low.defvjp(low_keep, low_pass)
low_back.defvjp(back_keep, back_low)

def rotate(tensor, places):
    half_rot = ROT // 2
    freqs = BASE ** (-(jnp.arange(half_rot, dtype=jnp.float32) * 2.0) / ROT)
    angles = places.astype(jnp.float32)[:, None] * freqs[None, :]
    cosine = jnp.cos(angles)[:, None, :]
    sine = jnp.sin(angles)[:, None, :]
    first_half = tensor[..., :half_rot]
    second_half = tensor[..., half_rot:ROT]
    return jnp.concatenate([first_half * cosine - second_half * sine, second_half * cosine + first_half * sine, tensor[..., ROT:]], axis=-1)

def layer_norm(values, gain, shift):
    center = values - lax.optimization_barrier(jnp.mean(values, -1, keepdims=True))
    spread = lax.optimization_barrier(jnp.mean(center * center, -1, keepdims=True))
    return center * lax.rsqrt(spread + EPS) * gain + shift

def matmul(left, right):
    return jnp.dot(left, right, precision=lax.Precision.HIGHEST, preferred_element_type=jnp.float32)

def attention(queries, keys, values):
    block = math.gcd(LEN, 512)
    query_blocks = queries.reshape(LEN // block, block, HEADS, HEAD_DIM)
    block_starts = (jnp.arange(LEN // block) * block).astype(jnp.int32)
    columns = jnp.arange(LEN).astype(jnp.int32)

    def one_block(inputs):
        query_block, block_start = inputs
        rows_here = block_start + jnp.arange(block).astype(jnp.int32)
        logits = jnp.einsum('qhd,khd->hqk', query_block, keys, precision=lax.Precision.HIGHEST) * float(HEAD_DIM) ** (-0.5)
        logits = jnp.where(columns[None, None, :] <= rows_here[None, :, None], logits, NEG)
        logits = low_back(logits)
        peak = lax.optimization_barrier(jnp.max(logits, -1, keepdims=True))
        expo = jnp.exp(logits - peak)
        probs = expo / lax.optimization_barrier(jnp.sum(expo, -1, keepdims=True))
        return jnp.einsum('hqk,khd->qhd', low(probs), values, precision=lax.Precision.HIGHEST)
    mixed = lax.map(jax.checkpoint(one_block), (query_blocks, block_starts))
    return mixed.reshape(LEN, HEADS * HEAD_DIM)

def layer(tokens, places, gain_one, shift_one, w_qkv, b_qkv, w_out, gain_two, shift_two, w_gate, w_up, w_down):
    normed = low(layer_norm(tokens, gain_one, shift_one))
    projected = low_back(matmul(normed, w_qkv) + b_qkv)
    queries = projected[:, :D].reshape(LEN, HEADS, HEAD_DIM)
    keys = projected[:, D:2 * D].reshape(LEN, HEADS, HEAD_DIM)
    values = projected[:, 2 * D:].reshape(LEN, HEADS, HEAD_DIM)
    queries = low(rotate(queries, places))
    keys = low(rotate(keys, places))
    values = low(values)
    mixed = low(low_back(attention(queries, keys, values)))
    middle = tokens + low_back(matmul(mixed, w_out))
    normed_two = low(layer_norm(middle, gain_two, shift_two))
    gate = low_back(matmul(normed_two, w_gate))
    upward = low_back(matmul(normed_two, w_up))
    hidden = low(jax.nn.silu(gate) * upward)
    return middle + low_back(matmul(hidden, w_down))

def reference(hidden_in, positions, languages, ln1_gain, ln1_bias, w_qkv, b_qkv, w_out, ln2_gain, ln2_bias, w_gate, w_up, w_down, cotangent):
    weights = tuple((item.astype(jnp.float32) for item in (ln1_gain, ln1_bias, w_qkv, b_qkv, w_out, ln2_gain, ln2_bias, w_gate, w_up, w_down)))
    matches = (languages[:, None] == jnp.arange(LANGS).astype(jnp.int32)[None, :]).astype(jnp.int32)
    counts = lax.optimization_barrier(jnp.sum(matches, 0))
    row_count = lax.optimization_barrier(jnp.sum(matches * counts[None, :], 1))
    row_weight = jnp.float32(ROWS * LEN) / (LANGS * (row_count * LEN).astype(jnp.float32))

    def one_row(carry, inputs):
        tokens, places, cot_row, weight_here = inputs

        def forward(tokens_in, *params):
            return layer(tokens_in, places, *params)
        result, pullback = jax.vjp(forward, tokens, *weights)
        grads = pullback(cot_row * weight_here)
        summed = tuple((old + new for old, new in zip(carry, grads[1:])))
        return (summed, (result.astype(jnp.bfloat16), grads[0].astype(jnp.bfloat16)))
    start_grads = tuple((jnp.zeros_like(item) for item in weights))
    totals, (output, input_grad) = lax.scan(one_row, start_grads, (hidden_in.astype(jnp.float32), positions, cotangent.astype(jnp.float32), row_weight))
    return (output, input_grad, totals[0], totals[1], totals[2], totals[3], totals[4], totals[5], totals[6], totals[7], totals[8], totals[9])
```

```python
import jax
import jax.numpy as jnp
from jax import lax
from jax.experimental import pallas as pl
from jax.experimental.pallas import tpu as pltpu
from jax.sharding import PartitionSpec as P

HEAD_DIM = 64
ROT = 16
LANGS = 7
CORES = 2
LANES = 128
QBLOCK = 256

EPS = 1e-05
NEG = -1e30
BASE = 10000.0

F32 = jnp.float32
BF16 = jnp.bfloat16


def standardize(values):
    center = values - jnp.mean(values, -1, keepdims=True)
    spread = jnp.mean(center * center, -1, keepdims=True)
    inverse = lax.rsqrt(spread + EPS)
    return (center * inverse, inverse)


def norm_back(grad_normed, normed, inverse):
    return inverse * (
        grad_normed
        - jnp.mean(grad_normed, -1, keepdims=True)
        - normed * jnp.mean(grad_normed * normed, -1, keepdims=True)
    )


def mm(left, right, dims=((1,), (0,))):
    return lax.dot_general(left, right, (dims, ((), ())), preferred_element_type=F32)


def pick(array, at, axis=0):
    return lax.dynamic_index_in_dim(array, at, axis, keepdims=False)


def rows_of(array, start, size):
    return lax.dynamic_slice_in_dim(array, start, size, 0)


def swap_cores(value):
    size = lax.axis_size("seq")
    return lax.ppermute(value, "seq", [(d, d ^ 1) for d in range(size)])


def ring(value):
    size = lax.axis_size("seq")
    return lax.ppermute(value, "seq", [(d, (d + CORES) % size) for d in range(size)])


def gather_tokens(local):
    size = lax.axis_size("seq")
    me = lax.axis_index("seq")
    chips = size // CORES
    chip, core = me // CORES, me % CORES
    count = local.shape[0]
    full = jnp.zeros((size * count,) + local.shape[1:], local.dtype)
    piece = local
    for step in range(chips):
        following = ring(piece) if step + 1 < chips else None
        other = swap_cores(piece)
        base = ((chip - step) % chips) * CORES
        full = lax.dynamic_update_slice_in_dim(full, piece, (base + core) * count, 0)
        full = lax.dynamic_update_slice_in_dim(full, other, (base + 1 - core) * count, 0)
        piece = following
    return full


def scatter_tokens(block_of, count):
    size = lax.axis_size("seq")
    me = lax.axis_index("seq")
    chips = size // CORES
    chip, core = me // CORES, me % CORES
    carried = None
    for step in range(1, chips + 1):
        block = block_of(((chip - step) % chips) * CORES * count)
        other = swap_cores(rows_of(block, (1 - core) * count, count).astype(BF16))
        total = rows_of(block, core * count, count) + other.astype(F32)
        if carried is not None:
            total = total + carried.astype(F32)
        if step < chips:
            carried = ring(total.astype(BF16))
    return total


def row_bits():
    size = lax.axis_size("row")
    return [1 << b for b in range(size.bit_length() - 1)]


def row_swap(value, bit):
    size = lax.axis_size("row")
    return lax.ppermute(value, "row", [(d, d ^ bit) for d in range(size)])


def flows_of():
    bits = row_bits()
    count = min(max(len(bits), 1), 2)
    return [bits[f:] + bits[:f] for f in range(count)]


def row_scatter(value):
    size = lax.axis_size("row")
    mine = lax.axis_index("row")
    flows = flows_of()
    total, columns = value.shape
    depth = len(row_bits())
    parts = value.reshape((len(flows),) + (2,) * depth + (total // (len(flows) * size), columns))
    done = []
    for number, order in enumerate(flows):
        part = parts[number]
        axes = [1 << (depth - 1 - a) for a in range(depth)]
        for bit in order:
            axis = axes.index(bit)
            own = (mine // bit) % 2
            sent = row_swap(pick(part, 1 - own, axis), bit)
            part = (pick(part, own, axis).astype(F32) + sent.astype(F32)).astype(value.dtype)
            axes.pop(axis)
        done.append(part)
    return jnp.stack(done)


def row_gather(chunks):
    mine = lax.axis_index("row")
    flows = flows_of()
    whole = []
    for number, order in enumerate(flows):
        part = chunks[number]
        axes = []
        for bit in reversed(order):
            other = row_swap(part, bit)
            own = (mine // bit) % 2
            at = len([b for b in axes if b > bit])
            low, high = jnp.where(own == 0, part, other), jnp.where(own == 0, other, part)
            part = jnp.stack([low, high], at)
            axes.insert(at, bit)
        whole.append(part.reshape((-1, chunks.shape[-1])))
    return jnp.concatenate(whole, 0)


def own_chunks(value):
    size = lax.axis_size("row")
    mine = lax.axis_index("row")
    flows = len(flows_of())
    total, columns = value.shape
    return pick(value.reshape(flows, size, total // (flows * size), columns), mine, 1)


def to_heads(units):
    size = lax.axis_size("seq")
    me = lax.axis_index("seq")
    unit = units.shape[-1] // 3
    got = jnp.stack(
        [
            lax.ppermute(
                units[..., i * unit : (i + 1) * unit],
                "seq",
                [(d, (3 * d + i) % size) for d in range(size)],
            )
            for i in range(3)
        ]
    )
    return [pick(got, (me + part * size) % 3) for part in range(3)]


def from_heads(parts):
    size = lax.axis_size("seq")
    me = lax.axis_index("seq")
    stacked = jnp.stack(parts)
    back = []
    for i in range(3):
        part = ((i - me) * pow(size, -1, 3)) % 3
        back.append(
            lax.ppermute(
                pick(stacked, part), "seq", [((3 * d + i) % size, d) for d in range(size)]
            )
        )
    return jnp.concatenate(back, -1)


def small_sums(values):
    size = lax.axis_size("seq")
    me = lax.axis_index("seq")
    part = values
    bit = size // 2
    while bit:
        own = (me // bit) % 2
        halves = part.reshape((2, part.shape[0] // 2) + part.shape[1:])
        part = pick(halves, own) + lax.ppermute(
            pick(halves, 1 - own), "seq", [(d, d ^ bit) for d in range(size)]
        )
        bit //= 2
    part = part[0]
    for bit in row_bits():
        part = part + row_swap(part, bit)
    return part


def turn(value, cosine, sine_low, sine_high):
    return (
        value * cosine
        + pltpu.roll(value, LANES - ROT // 2, 1) * sine_low
        + pltpu.roll(value, ROT // 2, 1) * sine_high
    )


def rotary_tables(places):
    half = ROT // 2
    freqs = BASE ** (-(jnp.arange(half, dtype=F32) * 2.0) / ROT)
    angles = places.astype(F32)[:, None] * freqs[None, :]
    cosine, sine = jnp.cos(angles), jnp.sin(angles)
    count = places.shape[0]
    none = jnp.zeros((count, HEAD_DIM - ROT), F32)
    zero = jnp.zeros((count, half), F32)
    repeat = LANES // HEAD_DIM

    def lanes(parts):
        return jnp.concatenate(parts * repeat, 1)

    return (
        lanes([cosine, cosine, none + 1.0]),
        lanes([-sine, zero, none]),
        lanes([zero, sine, none]),
    )


def head_masks(rows):
    lane = lax.broadcasted_iota(jnp.int32, (rows, LANES), 1)
    return [lane // HEAD_DIM == h for h in range(LANES // HEAD_DIM)]


def causal(first, rows, keys):
    query = lax.broadcasted_iota(jnp.int32, (rows, keys), 0) + first
    key = lax.broadcasted_iota(jnp.int32, (rows, keys), 1)
    return key <= query


ROWS_COLS = ((1,), (1,))
COLS_COLS = ((0,), (0,))


def attend_kernel(
    q_in, k_in, v_in, bias, cosine, sine_low, sine_high, out, q_out, k_out, v_out, stats
):
    length = q_in.shape[1]
    factor = float(HEAD_DIM) ** (-0.5)
    cos, low, high = cosine[...], sine_low[...], sine_high[...]
    q_out[0] = turn(q_in[0] + bias[0, 0:1], cos, low, high).astype(BF16)
    k_out[0] = turn(k_in[0] + bias[0, 1:2], cos, low, high).astype(BF16)
    v_out[0] = (v_in[0] + bias[0, 2:3]).astype(BF16)
    masks = head_masks(QBLOCK)
    for start in range(0, length, QBLOCK):
        end = start + QBLOCK
        query = q_out[0, start:end]
        key, value = k_out[0, 0:end], v_out[0, 0:end]
        keep = causal(start, QBLOCK, end)
        mixed, logs = None, None
        for mask in masks:
            logits = mm(jnp.where(mask, query, jnp.zeros_like(query)), key, ROWS_COLS) * factor
            logits = jnp.where(keep, logits, NEG)
            peak = jnp.max(logits, -1, keepdims=True)
            expo = jnp.exp(logits - peak)
            denom = jnp.sum(expo, -1, keepdims=True)
            part = mm((expo / denom).astype(BF16), value)
            log = jnp.broadcast_to(peak + jnp.log(denom), (QBLOCK, LANES))
            mixed = part if mixed is None else jnp.where(mask, part, mixed)
            logs = log if logs is None else jnp.where(mask, log, logs)
        out[0, start:end] = mixed.astype(BF16)
        stats[0, start:end] = logs


def attend_back_kernel(
    q_in, k_in, v_in, grad_in, stats, cosine, sine_low, sine_high, dq_out, dk_out, dv_out, dk, dv
):
    length = q_in.shape[1]
    factor = float(HEAD_DIM) ** (-0.5)
    cos, low, high = cosine[...], -sine_low[...], -sine_high[...]
    masks = head_masks(QBLOCK)
    dk[...] = jnp.zeros_like(dk)
    dv[...] = jnp.zeros_like(dv)
    for start in range(0, length, QBLOCK):
        end = start + QBLOCK
        query, grad = q_in[0, start:end], grad_in[0, start:end]
        key, value = k_in[0, 0:end], v_in[0, 0:end]
        keep = causal(start, QBLOCK, end)
        dq = None
        for number, mask in enumerate(masks):
            own_query = jnp.where(mask, query, jnp.zeros_like(query))
            own_grad = jnp.where(mask, grad, jnp.zeros_like(grad))
            log = stats[0, start:end, number * HEAD_DIM : number * HEAD_DIM + 1]
            logits = mm(own_query, key, ROWS_COLS) * factor
            probs = jnp.where(keep, jnp.exp(jnp.where(keep, logits, NEG) - log), 0.0)
            grad_probs = mm(own_grad, value, ROWS_COLS)
            inner = jnp.sum(grad_probs * probs, -1, keepdims=True)
            grad_logits = (probs * (grad_probs - inner)).astype(BF16)
            dv[0:end] += mm(probs.astype(BF16), own_grad, COLS_COLS)
            dk[0:end] += mm(grad_logits, own_query, COLS_COLS)
            part = mm(grad_logits, key)
            dq = part if dq is None else jnp.where(mask, part, dq)
        dq_out[0, start:end] = turn(
            dq * factor, cos[start:end], low[start:end], high[start:end]
        ).astype(BF16)
    dk_out[0] = turn(dk[...] * factor, cos, low, high).astype(BF16)
    dv_out[0] = dv[...].astype(BF16)


def pair_spec(length):
    return pl.BlockSpec((1, length, LANES), lambda g: (0, 0, g))


def attend(parts, bias, tables):
    _, length, width = parts[0].shape
    spec = pair_spec(length)
    table = pl.BlockSpec((length, LANES), lambda g: (0, 0))
    shape = jax.ShapeDtypeStruct((1, length, width), BF16)
    return pl.pallas_call(
        attend_kernel,
        grid=(width // LANES,),
        in_specs=[spec] * 3
        + [pl.BlockSpec((1, 3, LANES), lambda g: (0, 0, g))]
        + [table] * 3,
        out_specs=[spec] * 5,
        out_shape=[shape] * 4 + [jax.ShapeDtypeStruct((1, length, width), F32)],
        name="attend",
    )(*parts, bias, *tables)


def attend_back(rotated, grad, stats, tables):
    _, length, width = grad.shape
    spec = pair_spec(length)
    table = pl.BlockSpec((length, LANES), lambda g: (0, 0))
    shape = jax.ShapeDtypeStruct((1, length, width), BF16)
    return pl.pallas_call(
        attend_back_kernel,
        grid=(width // LANES,),
        in_specs=[spec] * 5 + [table] * 3,
        out_specs=[spec] * 3,
        out_shape=[shape] * 3,
        scratch_shapes=[pltpu.VMEM((length, LANES), F32)] * 2,
        name="attend_back",
    )(*rotated, grad, stats, *tables)


def body(
    hidden_in,
    positions,
    languages,
    ln1_gain,
    ln1_bias,
    w_qkv,
    b_qkv,
    w_out,
    ln2_gain,
    ln2_bias,
    w_gate,
    w_up,
    w_down,
    cotangent,
):
    tokens = hidden_in[0].astype(F32)
    count, width = tokens.shape
    size = lax.axis_size("seq")
    length = count * size
    unit = width // size
    language_ids = jnp.arange(LANGS, dtype=jnp.int32)
    marks_all = (languages[:, None] == language_ids[None, :]).astype(jnp.int32)
    language_totals = jnp.sum(marks_all, 0)
    own_language = lax.dynamic_slice_in_dim(languages, lax.axis_index("row"), 1, 0)
    own_marks = (own_language[0] == language_ids).astype(jnp.int32)
    own_count = jnp.sum(own_marks * language_totals)
    row_weight = F32(languages.shape[0] * length) / (LANGS * (own_count * length).astype(F32))
    gain_one, shift_one = ln1_gain.astype(F32), ln1_bias.astype(F32)
    gain_two, shift_two = ln2_gain.astype(F32), ln2_bias.astype(F32)

    normed_one, inverse_one = standardize(tokens)
    first_in = (normed_one * gain_one + shift_one).astype(BF16)
    heads_w = jnp.concatenate(to_heads(own_chunks(w_qkv)), -1)
    heads_w = row_gather(heads_w)
    heads_b = jnp.stack(to_heads(b_qkv))[None].astype(F32)
    places = gather_tokens(positions[0])
    tables = rotary_tables(places)
    first_full = gather_tokens(first_in)
    projected = mm(first_full, heads_w)
    parts = [projected[None, :, i * unit : (i + 1) * unit] for i in range(3)]
    mixed, *rotated, stats = attend(parts, heads_b, tables)
    mixed = mixed[0]
    middle = tokens + scatter_tokens(
        lambda row: mm(rows_of(mixed, row, CORES * count), w_out), count
    )

    normed_two, inverse_two = standardize(middle)
    second_in = (normed_two * gain_two + shift_two).astype(BF16)
    grad_top = cotangent[0].astype(F32) * row_weight
    grad_top_full = gather_tokens(grad_top.astype(BF16))
    second_full = gather_tokens(second_in)
    gate = mm(second_full, w_gate)
    upward = mm(second_full, w_up)
    sigmoid_gate = jax.nn.sigmoid(gate)
    activated = gate * sigmoid_gate
    hidden = (activated * upward).astype(BF16)
    grad_hidden = mm(grad_top_full, w_down, ROWS_COLS)
    slope = sigmoid_gate * (1.0 + gate * (1.0 - sigmoid_gate))
    grad_gate = (grad_hidden * upward * slope).astype(BF16)
    grad_upward = (grad_hidden * activated).astype(BF16)
    feed_out = scatter_tokens(lambda row: mm(rows_of(hidden, row, CORES * count), w_down), count)
    output = (middle + feed_out).astype(BF16)[None]

    grad_second = scatter_tokens(
        lambda row: mm(rows_of(grad_gate, row, CORES * count), w_gate, ROWS_COLS)
        + mm(rows_of(grad_upward, row, CORES * count), w_up, ROWS_COLS),
        count,
    )
    feed_grads = lax.psum(
        (
            mm(second_full, grad_gate, COLS_COLS).astype(BF16),
            mm(second_full, grad_upward, COLS_COLS).astype(BF16),
            mm(hidden, grad_top_full, COLS_COLS).astype(BF16),
        ),
        "row",
    )
    grad_middle = grad_top + norm_back(grad_second * gain_two, normed_two, inverse_two)
    grad_middle_full = gather_tokens(grad_middle.astype(BF16))
    grad_mixed = mm(grad_middle_full, w_out, ROWS_COLS).astype(BF16)
    grad_w_out = mm(mixed, grad_middle_full, COLS_COLS).astype(BF16)
    grad_w_out = row_gather(row_scatter(grad_w_out)).astype(F32)
    grad_parts = attend_back(rotated, grad_mixed[None], stats, tables)
    grad_projected = jnp.concatenate([part[0] for part in grad_parts], 1)
    grad_b = jnp.sum(grad_projected.astype(F32), 0)
    grad_first = scatter_tokens(
        lambda row: mm(rows_of(grad_projected, row, CORES * count), heads_w, ROWS_COLS), count
    )
    grad_w_qkv = row_scatter(mm(first_full, grad_projected, COLS_COLS).astype(BF16))
    grad_w_qkv = from_heads([grad_w_qkv[..., i * unit : (i + 1) * unit] for i in range(3)])
    grad_w_qkv = row_gather(grad_w_qkv).astype(F32)
    input_grad = (grad_middle + norm_back(grad_first * gain_one, normed_one, inverse_one)).astype(
        BF16
    )[None]

    def shards(vector):
        return vector.reshape(size, -1)

    early = small_sums(
        jnp.concatenate(
            [shards(jnp.sum(grad_second * normed_two, 0)), shards(jnp.sum(grad_second, 0))], 1
        )
    )
    late = small_sums(
        jnp.concatenate(
            [shards(jnp.sum(grad_first * normed_one, 0)), shards(jnp.sum(grad_first, 0))], 1
        )
    )
    for bit in row_bits():
        grad_b = grad_b + row_swap(grad_b, bit)
    grad_b = from_heads([grad_b[i * unit : (i + 1) * unit] for i in range(3)])
    return (
        output,
        input_grad,
        late[:unit],
        late[unit:],
        grad_w_qkv,
        grad_b,
        grad_w_out,
        early[:unit],
        early[unit:],
        feed_grads[0].astype(F32),
        feed_grads[1].astype(F32),
        feed_grads[2].astype(F32),
    )


def solution(mesh):
    placed = (
        P("row", "seq", None),
        P("row", "seq"),
        P(),
        P(),
        P(),
        P(None, "seq"),
        P("seq"),
        P("seq", None),
        P(),
        P(),
        P(None, "seq"),
        P(None, "seq"),
        P("seq", None),
        P("row", "seq", None),
    )
    return jax.shard_map(
        body,
        mesh=mesh,
        in_specs=placed,
        out_specs=(
            P("row", "seq", None),
            P("row", "seq", None),
            P("seq"),
            P("seq"),
            P(None, "seq"),
            P("seq"),
            P("seq", None),
            P("seq"),
            P("seq"),
            P(None, "seq"),
            P(None, "seq"),
            P("seq", None),
        ),
        check_vma=False,
    )
```

```python
import jax
import jax.numpy as jnp
from jax import lax
from jax.experimental import pallas as pl
from jax.experimental.pallas import tpu as pltpu
from jax.sharding import PartitionSpec as P


HEAD_DIM = 64
ROT = 16
LANGS = 7
CORES = 2
LANES = 128
QBLOCK = 256
SPLITS = 2
BIAS_ROWS = 16

EPS = 1e-05
NEG = -1e30
BASE = 10000.0

F32 = jnp.float32
BF16 = jnp.bfloat16


def standardize(values):
    center = values - jnp.mean(values, -1, keepdims=True)
    spread = jnp.mean(center * center, -1, keepdims=True)
    inverse = lax.rsqrt(spread + EPS)
    return (center * inverse, inverse)


def norm_back(grad_normed, normed, inverse):
    return inverse * (
        grad_normed
        - jnp.mean(grad_normed, -1, keepdims=True)
        - normed * jnp.mean(grad_normed * normed, -1, keepdims=True)
    )


def mm(left, right, dims=((1,), (0,))):
    return lax.dot_general(left, right, (dims, ((), ())), preferred_element_type=F32)


def pick(array, at, axis=0):
    return lax.dynamic_index_in_dim(array, at, axis, keepdims=False)


def rows_of(array, start, size):
    return lax.dynamic_slice_in_dim(array, start, size, 0)


def swap_cores(value):
    size = lax.axis_size("seq")
    return lax.ppermute(value, "seq", [(d, d ^ 1) for d in range(size)])


def ring(value):
    size = lax.axis_size("seq")
    to = [(d, (d + CORES) % size) for d in range(size)]
    return [lax.ppermute(part, "seq", to) for part in value]


def cut(value):
    rows = value.shape[0] // SPLITS
    return [value[k * rows : (k + 1) * rows] for k in range(SPLITS)]


def after(value, *earlier):
    return lax.optimization_barrier((value,) + earlier)[0]


def gather_places(local):
    size = lax.axis_size("seq")
    me = lax.axis_index("seq")
    have, bit = local, 1
    while bit < size:
        other = lax.ppermute(have, "seq", [(d, d ^ bit) for d in range(size)])
        own = (me // bit) % 2
        have = jnp.where(
            own == 0, jnp.concatenate([have, other]), jnp.concatenate([other, have])
        )
        bit *= 2
    return have


def gather_tokens(local):
    size = lax.axis_size("seq")
    me = lax.axis_index("seq")
    chips = size // CORES
    chip, core = me // CORES, me % CORES
    count = local.shape[0]
    full = jnp.zeros((size * count,) + local.shape[1:], local.dtype)
    piece = cut(local)
    for step in range(chips):
        following = ring(piece) if step + 1 < chips else None
        base = ((chip - step) % chips) * CORES
        rows = count // SPLITS
        for k, part in enumerate(piece):
            other = swap_cores(part)
            full = lax.dynamic_update_slice_in_dim(full, part, (base + core) * count + k * rows, 0)
            full = lax.dynamic_update_slice_in_dim(
                full, other, (base + 1 - core) * count + k * rows, 0
            )
        piece = following
    return full


def scatter_tokens(block_of, count, meanwhile=None):
    size = lax.axis_size("seq")
    me = lax.axis_index("seq")
    chips = size // CORES
    chip, core = me // CORES, me % CORES
    rows = count // SPLITS
    carried = [None] * SPLITS
    for step in range(1, chips + 1):
        row = ((chip - step) % chips) * CORES * count
        if meanwhile is not None and step == 2:
            row = after(row, *meanwhile)
        block = block_of(row)
        totals = []
        for k in range(SPLITS):
            other = swap_cores(rows_of(block, (1 - core) * count + k * rows, rows).astype(BF16))
            total = rows_of(block, core * count + k * rows, rows) + other.astype(F32)
            if carried[k] is not None:
                total = total + carried[k].astype(F32)
            totals.append(total)
        if step < chips:
            carried = ring([total.astype(BF16) for total in totals])
    return jnp.concatenate(totals, 0)


def row_bits():
    size = lax.axis_size("row")
    return [1 << b for b in range(size.bit_length() - 1)]


def row_swap(value, bit):
    size = lax.axis_size("row")
    return lax.ppermute(value, "row", [(d, d ^ bit) for d in range(size)])


def side(bit):
    return (lax.axis_index("row") // bit) % 2


def flows_of():
    bits = row_bits()
    return [bits, bits[1:] + bits[:1]] if len(bits) > 1 else [bits]


def place_in(order):
    place = 0
    for bit in order:
        place = place * 2 + side(bit)
    return place


def row_scatter(value):
    flows = flows_of()
    done = []
    for number, order in enumerate(flows):
        rows = value.shape[0] // len(flows)
        part = value[number * rows : (number + 1) * rows]
        for bit in order:
            half = part.shape[0] // 2
            sent = row_swap(rows_of(part, (1 - side(bit)) * half, half), bit)
            kept = rows_of(part, side(bit) * half, half)
            part = (kept.astype(F32) + sent.astype(F32)).astype(value.dtype)
        done.append(part)
    return done


def row_gather(chunks, dtype):
    flows = flows_of()
    rows, columns = chunks[0].shape
    total = rows * lax.axis_size("row")
    full = jnp.zeros((total * len(flows), columns), dtype)
    for number, order in enumerate(flows):
        pieces = [(place_in(order), chunks[number])]
        for level, bit in enumerate(reversed(order)):
            flip = (1 - 2 * side(bit)) << level
            pieces = pieces + [(at + flip, row_swap(piece, bit)) for at, piece in pieces]
        for at, piece in pieces:
            full = lax.dynamic_update_slice_in_dim(
                full, piece.astype(dtype), number * total + at * rows, 0
            )
    return full


def own_chunks(value):
    flows = flows_of()
    total = value.shape[0] // len(flows)
    rows = total // lax.axis_size("row")
    return [
        rows_of(value, number * total + place_in(order) * rows, rows)
        for number, order in enumerate(flows)
    ]


def to_heads(units):
    size = lax.axis_size("seq")
    me = lax.axis_index("seq")
    unit = units.shape[-1] // 3
    got = jnp.stack(
        [
            lax.ppermute(
                units[..., i * unit : (i + 1) * unit],
                "seq",
                [(d, (3 * d + i) % size) for d in range(size)],
            )
            for i in range(3)
        ]
    )
    return [pick(got, (me + part * size) % 3) for part in range(3)]


def from_heads(parts):
    size = lax.axis_size("seq")
    me = lax.axis_index("seq")
    stacked = jnp.stack(parts)
    back = []
    for i in range(3):
        part = ((i - me) * pow(size, -1, 3)) % 3
        back.append(
            lax.ppermute(
                pick(stacked, part), "seq", [((3 * d + i) % size, d) for d in range(size)]
            )
        )
    return jnp.concatenate(back, -1)


def small_sums(values):
    size = lax.axis_size("seq")
    me = lax.axis_index("seq")
    part = values
    bit = size // 2
    while bit:
        own = (me // bit) % 2
        halves = part.reshape((2, part.shape[0] // 2) + part.shape[1:])
        part = pick(halves, own) + lax.ppermute(
            pick(halves, 1 - own), "seq", [(d, d ^ bit) for d in range(size)]
        )
        bit //= 2
    part = part[0]
    for bit in row_bits():
        part = part + row_swap(part, bit)
    return part


def turn(value, cosine, sine):
    lane = lax.broadcasted_iota(jnp.int32, sine.shape, 1) % HEAD_DIM
    half = ROT // 2
    low = jnp.where(lane < half, -sine, 0.0)
    high = jnp.where(lane < half, 0.0, sine)
    return (
        value * cosine
        + pltpu.roll(value, LANES - half, 1) * low
        + pltpu.roll(value, half, 1) * high
    )


def rotary_tables(places):
    half = ROT // 2
    freqs = BASE ** (-(jnp.arange(half, dtype=F32) * 2.0) / ROT)
    still = jnp.zeros(HEAD_DIM - ROT, F32)
    lanes = jnp.tile(jnp.concatenate([freqs, freqs, still]), LANES // HEAD_DIM)
    angles = places.astype(F32)[:, None] * lanes[None, :]
    return jnp.cos(angles), jnp.sin(angles)


def head_masks(rows):
    lane = lax.broadcasted_iota(jnp.int32, (rows, LANES), 1)
    return [lane // HEAD_DIM == h for h in range(LANES // HEAD_DIM)]


def causal(first, rows, keys):
    query = lax.broadcasted_iota(jnp.int32, (rows, keys), 0) + first
    key = lax.broadcasted_iota(jnp.int32, (rows, keys), 1)
    return key <= query


ROWS_COLS = ((1,), (1,))
COLS_COLS = ((0,), (0,))


def attend_kernel(
    q_in, k_in, v_in, bias, cosine, sine, out, q_out, k_out, v_out, stats
):
    length = q_in.shape[1]
    factor = float(HEAD_DIM) ** (-0.5)
    cos, sin = cosine[...], sine[...]
    q_out[0] = turn(q_in[0] + bias[0, 0:1], cos, sin).astype(BF16)
    k_out[0] = turn(k_in[0] + bias[0, 1:2], cos, sin).astype(BF16)
    v_out[0] = (v_in[0] + bias[0, 2:3]).astype(BF16)
    masks = head_masks(QBLOCK)
    for start in range(0, length, QBLOCK):
        end = start + QBLOCK
        query = q_out[0, start:end]
        key, value = k_out[0, 0:end], v_out[0, 0:end]
        keep = causal(start, QBLOCK, end)
        mixed, logs = None, None
        for mask in masks:
            logits = mm(jnp.where(mask, query, jnp.zeros_like(query)), key, ROWS_COLS) * factor
            logits = jnp.where(keep, logits, NEG)
            peak = jnp.max(logits, -1, keepdims=True)
            expo = jnp.exp(logits - peak)
            denom = jnp.sum(expo, -1, keepdims=True)
            part = mm((expo / denom).astype(BF16), value)
            log = jnp.broadcast_to(peak + jnp.log(denom), (QBLOCK, LANES))
            mixed = part if mixed is None else jnp.where(mask, part, mixed)
            logs = log if logs is None else jnp.where(mask, log, logs)
        out[0, start:end] = mixed.astype(BF16)
        stats[0, start:end] = logs


def attend_back_kernel(
    q_in, k_in, v_in, grad_in, stats, cosine, sine, dq_out, dk_out, dv_out, dk, dv
):
    length = q_in.shape[1]
    factor = float(HEAD_DIM) ** (-0.5)
    cos, sin = cosine[...], -sine[...]
    masks = head_masks(QBLOCK)
    dk[...] = jnp.zeros_like(dk)
    dv[...] = jnp.zeros_like(dv)
    for start in range(0, length, QBLOCK):
        end = start + QBLOCK
        query, grad = q_in[0, start:end], grad_in[0, start:end]
        key, value = k_in[0, 0:end], v_in[0, 0:end]
        keep = causal(start, QBLOCK, end)
        dq = None
        for number, mask in enumerate(masks):
            own_query = jnp.where(mask, query, jnp.zeros_like(query))
            own_grad = jnp.where(mask, grad, jnp.zeros_like(grad))
            log = stats[0, start:end, number * HEAD_DIM : number * HEAD_DIM + 1]
            logits = mm(own_query, key, ROWS_COLS) * factor
            probs = jnp.where(keep, jnp.exp(jnp.where(keep, logits, NEG) - log), 0.0)
            grad_probs = mm(own_grad, value, ROWS_COLS)
            inner = jnp.sum(grad_probs * probs, -1, keepdims=True)
            grad_logits = (probs * (grad_probs - inner)).astype(BF16)
            dv[0:end] += mm(probs.astype(BF16), own_grad, COLS_COLS)
            dk[0:end] += mm(grad_logits, own_query, COLS_COLS)
            part = mm(grad_logits, key)
            dq = part if dq is None else jnp.where(mask, part, dq)
        dq_out[0, start:end] = turn(dq * factor, cos[start:end], sin[start:end]).astype(BF16)
    dk_out[0] = turn(dk[...] * factor, cos, sin).astype(BF16)
    dv_out[0] = dv[...].astype(BF16)


def pair_spec(length):
    return pl.BlockSpec((1, length, LANES), lambda g: (0, 0, g))


def attend(parts, bias, tables):
    _, length, width = parts[0].shape
    spec = pair_spec(length)
    table = pl.BlockSpec((length, LANES), lambda g: (0, 0))
    shape = jax.ShapeDtypeStruct((1, length, width), BF16)
    return pl.pallas_call(
        attend_kernel,
        grid=(width // LANES,),
        in_specs=[spec] * 3
        + [pl.BlockSpec((1, 3, LANES), lambda g: (0, 0, g))]
        + [table] * 2,
        out_specs=[spec] * 5,
        out_shape=[shape] * 4 + [jax.ShapeDtypeStruct((1, length, width), F32)],
        name="attend",
    )(*parts, bias, *tables)


def attend_back(rotated, grad, stats, tables):
    _, length, width = grad.shape
    spec = pair_spec(length)
    table = pl.BlockSpec((length, LANES), lambda g: (0, 0))
    shape = jax.ShapeDtypeStruct((1, length, width), BF16)
    return pl.pallas_call(
        attend_back_kernel,
        grid=(width // LANES,),
        in_specs=[spec] * 5 + [table] * 2,
        out_specs=[spec] * 3,
        out_shape=[shape] * 3,
        scratch_shapes=[pltpu.VMEM((length, LANES), F32)] * 2,
        name="attend_back",
    )(*rotated, grad, stats, *tables)


def body(
    hidden_in,
    positions,
    languages,
    ln1_gain,
    ln1_bias,
    w_qkv,
    b_qkv,
    w_out,
    ln2_gain,
    ln2_bias,
    w_gate,
    w_up,
    w_down,
    cotangent,
):
    tokens = hidden_in[0].astype(F32)
    count, width = tokens.shape
    size = lax.axis_size("seq")
    length = count * size
    unit = width // size
    language_ids = jnp.arange(LANGS, dtype=jnp.int32)
    marks_all = (languages[:, None] == language_ids[None, :]).astype(jnp.int32)
    language_totals = jnp.sum(marks_all, 0)
    own_language = lax.dynamic_slice_in_dim(languages, lax.axis_index("row"), 1, 0)
    own_marks = (own_language[0] == language_ids).astype(jnp.int32)
    own_count = jnp.sum(own_marks * language_totals)
    row_weight = F32(languages.shape[0] * length) / (LANGS * (own_count * length).astype(F32))
    gain_one, shift_one = ln1_gain.astype(F32), ln1_bias.astype(F32)
    gain_two, shift_two = ln2_gain.astype(F32), ln2_bias.astype(F32)

    normed_one, inverse_one = standardize(tokens)
    first_in = (normed_one * gain_one + shift_one).astype(BF16)
    bias_rows = jnp.broadcast_to(b_qkv[None], (BIAS_ROWS,) + b_qkv.shape)
    moved = to_heads(jnp.concatenate(own_chunks(w_qkv) + [bias_rows], 0))
    flows = len(flows_of())
    heads_b = jnp.concatenate([part[-1:] for part in moved], 0)[None].astype(F32)
    moved = jnp.concatenate([part[:-BIAS_ROWS] for part in moved], -1)
    heads_w = row_gather(jnp.split(moved, flows, 0), BF16)
    places = gather_places(positions[0])
    tables = rotary_tables(places)
    first_full = lax.all_gather(first_in, "seq", axis=0, tiled=True)
    projected = mm(first_full, heads_w)
    parts = [projected[None, :, i * unit : (i + 1) * unit] for i in range(3)]
    mixed, *rotated, stats = attend(parts, heads_b, tables)
    mixed = mixed[0]
    middle = tokens + scatter_tokens(
        lambda row: mm(rows_of(mixed, row, CORES * count), w_out), count
    )

    normed_two, inverse_two = standardize(middle)
    second_in = (normed_two * gain_two + shift_two).astype(BF16)
    grad_top = cotangent[0].astype(F32) * row_weight
    grad_top_full = lax.all_gather(grad_top.astype(BF16), "seq", axis=0, tiled=True)
    second_full = gather_tokens(second_in)
    gate = mm(second_full, w_gate)
    upward = mm(second_full, w_up)
    sigmoid_gate = jax.nn.sigmoid(gate)
    activated = gate * sigmoid_gate
    hidden = (activated * upward).astype(BF16)
    grad_hidden = mm(grad_top_full, w_down, ROWS_COLS)
    slope = sigmoid_gate * (1.0 + gate * (1.0 - sigmoid_gate))
    grad_gate = (grad_hidden * upward * slope).astype(BF16)
    grad_upward = (grad_hidden * activated).astype(BF16)
    feed_grads = (
        mm(second_full, grad_gate, COLS_COLS).astype(BF16),
        mm(second_full, grad_upward, COLS_COLS).astype(BF16),
        mm(hidden, grad_top_full, COLS_COLS).astype(BF16),
    )
    grad_second = scatter_tokens(
        lambda row: mm(rows_of(grad_gate, row, CORES * count), w_gate, ROWS_COLS)
        + mm(rows_of(grad_upward, row, CORES * count), w_up, ROWS_COLS),
        count,
        feed_grads,
    )
    feed_grads = lax.psum(feed_grads, "row")
    grad_middle = grad_top + norm_back(grad_second * gain_two, normed_two, inverse_two)
    grad_middle_full = gather_tokens(grad_middle.astype(BF16))
    grad_mixed = mm(grad_middle_full, w_out, ROWS_COLS).astype(BF16)
    grad_w_out = lax.psum(
        after(mm(mixed, grad_middle_full, COLS_COLS).astype(BF16), *feed_grads), "row"
    ).astype(F32)
    grad_parts = attend_back(rotated, grad_mixed[None], stats, tables)
    grad_projected = jnp.concatenate([part[0] for part in grad_parts], 1)
    grad_b = jnp.sum(grad_projected.astype(F32), 0)
    grad_w_qkv = row_scatter(mm(first_full, grad_projected, COLS_COLS).astype(BF16))
    grad_w_qkv = jnp.concatenate(grad_w_qkv, 0)
    grad_w_qkv = from_heads([grad_w_qkv[:, i * unit : (i + 1) * unit] for i in range(3)])
    grad_w_qkv = row_gather(jnp.split(grad_w_qkv, flows, 0), F32)
    grad_first = scatter_tokens(
        lambda row: mm(rows_of(grad_projected, row, CORES * count), heads_w, ROWS_COLS), count
    )
    feed_out = scatter_tokens(lambda row: mm(rows_of(hidden, row, CORES * count), w_down), count)
    output = (middle + feed_out).astype(BF16)[None]
    input_grad = (grad_middle + norm_back(grad_first * gain_one, normed_one, inverse_one)).astype(
        BF16
    )[None]

    def shards(vector):
        return vector.reshape(size, -1)

    early = small_sums(
        jnp.concatenate(
            [shards(jnp.sum(grad_second * normed_two, 0)), shards(jnp.sum(grad_second, 0))], 1
        )
    )
    late = small_sums(
        jnp.concatenate(
            [shards(jnp.sum(grad_first * normed_one, 0)), shards(jnp.sum(grad_first, 0))], 1
        )
    )
    for bit in row_bits():
        grad_b = grad_b + row_swap(grad_b, bit)
    grad_b = from_heads([grad_b[i * unit : (i + 1) * unit] for i in range(3)])
    return (
        output,
        input_grad,
        late[:unit],
        late[unit:],
        grad_w_qkv,
        grad_b,
        grad_w_out,
        early[:unit],
        early[unit:],
        feed_grads[0].astype(F32),
        feed_grads[1].astype(F32),
        feed_grads[2].astype(F32),
    )


def solution(mesh):
    placed = (
        P("row", "seq", None),
        P("row", "seq"),
        P(),
        P(),
        P(),
        P(None, "seq"),
        P("seq"),
        P("seq", None),
        P(),
        P(),
        P(None, "seq"),
        P(None, "seq"),
        P("seq", None),
        P("row", "seq", None),
    )
    return jax.shard_map(
        body,
        mesh=mesh,
        in_specs=placed,
        out_specs=(
            P("row", "seq", None),
            P("row", "seq", None),
            P("seq"),
            P("seq"),
            P(None, "seq"),
            P("seq"),
            P("seq", None),
            P("seq"),
            P("seq"),
            P(None, "seq"),
            P(None, "seq"),
            P("seq", None),
        ),
        check_vma=False,
    )
```

```python
import jax
import jax.numpy as jnp
from jax import lax
from jax.experimental import pallas as pl
from jax.experimental.pallas import tpu as pltpu
from jax.sharding import PartitionSpec as P


HEAD_DIM = 64
ROT = 16
LANGS = 7
CORES = 2
LANES = 128
QBLOCK = 256
SPLITS = 2
BIAS_ROWS = 16

EPS = 1e-05
NEG = -1e30
BASE = 10000.0

F32 = jnp.float32
BF16 = jnp.bfloat16


def standardize(values):
    center = values - jnp.mean(values, -1, keepdims=True)
    spread = jnp.mean(center * center, -1, keepdims=True)
    inverse = lax.rsqrt(spread + EPS)
    return (center * inverse, inverse)


def norm_back(grad_normed, normed, inverse):
    return inverse * (
        grad_normed
        - jnp.mean(grad_normed, -1, keepdims=True)
        - normed * jnp.mean(grad_normed * normed, -1, keepdims=True)
    )


def mm(left, right, dims=((1,), (0,))):
    return lax.dot_general(left, right, (dims, ((), ())), preferred_element_type=F32)


def pick(array, at, axis=0):
    return lax.dynamic_index_in_dim(array, at, axis, keepdims=False)


def rows_of(array, start, size):
    return lax.dynamic_slice_in_dim(array, start, size, 0)


def swap_cores(value):
    size = lax.axis_size("seq")
    return lax.ppermute(value, "seq", [(d, d ^ 1) for d in range(size)])


def ring(value):
    size = lax.axis_size("seq")
    to = [(d, (d + CORES) % size) for d in range(size)]
    return [lax.ppermute(part, "seq", to) for part in value]


def cut(value):
    rows = value.shape[0] // SPLITS
    return [value[k * rows : (k + 1) * rows] for k in range(SPLITS)]


def after(value, *earlier):
    return lax.optimization_barrier((value,) + earlier)[0]


def gather_places(local):
    size = lax.axis_size("seq")
    me = lax.axis_index("seq")
    have, bit = local, 1
    while bit < size:
        other = lax.ppermute(have, "seq", [(d, d ^ bit) for d in range(size)])
        own = (me // bit) % 2
        have = jnp.where(
            own == 0, jnp.concatenate([have, other]), jnp.concatenate([other, have])
        )
        bit *= 2
    return have


def gather_tokens(local):
    size = lax.axis_size("seq")
    me = lax.axis_index("seq")
    chips = size // CORES
    chip, core = me // CORES, me % CORES
    count = local.shape[0]
    full = jnp.zeros((size * count,) + local.shape[1:], local.dtype)
    piece = cut(local)
    for step in range(chips):
        following = None
        if step + 1 < chips:
            following = ring(piece)
        base = ((chip - step) % chips) * CORES
        rows = count // SPLITS
        for k, part in enumerate(piece):
            other = swap_cores(part)
            full = lax.dynamic_update_slice_in_dim(full, part, (base + core) * count + k * rows, 0)
            full = lax.dynamic_update_slice_in_dim(
                full, other, (base + 1 - core) * count + k * rows, 0
            )
        piece = following
    return full


def scatter_tokens(block_of, count, meanwhile=None):
    size = lax.axis_size("seq")
    me = lax.axis_index("seq")
    chips = size // CORES
    chip, core = me // CORES, me % CORES
    rows = count // SPLITS
    carried = [None] * SPLITS
    for step in range(1, chips + 1):
        row = ((chip - step) % chips) * CORES * count
        if meanwhile is not None and step == 2:
            row = after(row, *meanwhile)
        block = block_of(row)
        totals = []
        for k in range(SPLITS):
            other = swap_cores(rows_of(block, (1 - core) * count + k * rows, rows).astype(BF16))
            total = rows_of(block, core * count + k * rows, rows) + other.astype(F32)
            if carried[k] is not None:
                total = total + carried[k].astype(F32)
            totals.append(total)
        if step < chips:
            carried = ring([total.astype(BF16) for total in totals])
    return jnp.concatenate(totals, 0)


def row_bits():
    size = lax.axis_size("row")
    return [1 << b for b in range(size.bit_length() - 1)]


def row_swap(value, bit):
    size = lax.axis_size("row")
    return lax.ppermute(value, "row", [(d, d ^ bit) for d in range(size)])


def side(bit):
    return (lax.axis_index("row") // bit) % 2


def flows_of():
    bits = row_bits()
    return [bits, bits[1:] + bits[:1]] if len(bits) > 1 else [bits]


def place_in(order):
    place = 0
    for bit in order:
        place = place * 2 + side(bit)
    return place


def row_scatter(value):
    flows = flows_of()
    done = []
    for number, order in enumerate(flows):
        rows = value.shape[0] // len(flows)
        part = value[number * rows : (number + 1) * rows]
        for bit in order:
            half = part.shape[0] // 2
            sent = row_swap(rows_of(part, (1 - side(bit)) * half, half), bit)
            kept = rows_of(part, side(bit) * half, half)
            part = (kept.astype(F32) + sent.astype(F32)).astype(value.dtype)
        done.append(part)
    return done


def row_pieces(chunks):
    rows = chunks[0].shape[0]
    total = rows * lax.axis_size("row")
    found = []
    for number, order in enumerate(flows_of()):
        pieces = [(place_in(order), chunks[number])]
        for level, bit in enumerate(reversed(order)):
            flip = (1 - 2 * side(bit)) << level
            pieces = pieces + [(at + flip, row_swap(piece, bit)) for at, piece in pieces]
        found += [(number * total + at * rows, piece) for at, piece in pieces]
    return found


def row_gather(chunks):
    pieces = row_pieces(chunks)
    full = jnp.zeros((chunks[0].shape[0] * len(pieces), chunks[0].shape[1]), chunks[0].dtype)
    for start, piece in pieces:
        full = lax.dynamic_update_slice_in_dim(full, piece, start, 0)
    return full


def own_chunks(value):
    flows = flows_of()
    total = value.shape[0] // len(flows)
    rows = total // lax.axis_size("row")
    return [
        rows_of(value, number * total + place_in(order) * rows, rows)
        for number, order in enumerate(flows)
    ]


def to_heads(units):
    size = lax.axis_size("seq")
    me = lax.axis_index("seq")
    unit = units.shape[-1] // 3
    got = jnp.stack(
        [
            lax.ppermute(
                units[..., i * unit : (i + 1) * unit],
                "seq",
                [(d, (3 * d + i) % size) for d in range(size)],
            )
            for i in range(3)
        ]
    )
    return [pick(got, (me + part * size) % 3) for part in range(3)]


def from_heads(parts):
    size = lax.axis_size("seq")
    me = lax.axis_index("seq")
    stacked = jnp.stack(parts)
    back = []
    for i in range(3):
        part = ((i - me) * pow(size, -1, 3)) % 3
        back.append(
            lax.ppermute(
                pick(stacked, part), "seq", [((3 * d + i) % size, d) for d in range(size)]
            )
        )
    return jnp.concatenate(back, -1)


def small_sums(values):
    size = lax.axis_size("seq")
    me = lax.axis_index("seq")
    part = values
    bit = size // 2
    while bit:
        own = (me // bit) % 2
        halves = part.reshape((2, part.shape[0] // 2) + part.shape[1:])
        part = pick(halves, own) + lax.ppermute(
            pick(halves, 1 - own), "seq", [(d, d ^ bit) for d in range(size)]
        )
        bit //= 2
    part = part[0]
    for bit in row_bits():
        part = part + row_swap(part, bit)
    return part


def turn(value, cosine, sine):
    lane = lax.broadcasted_iota(jnp.int32, sine.shape, 1) % HEAD_DIM
    half = ROT // 2
    low = jnp.where(lane < half, -sine, 0.0)
    high = jnp.where(lane < half, 0.0, sine)
    return (
        value * cosine
        + pltpu.roll(value, LANES - half, 1) * low
        + pltpu.roll(value, half, 1) * high
    )


def rotary_tables(places):
    half = ROT // 2
    freqs = BASE ** (-(jnp.arange(half, dtype=F32) * 2.0) / ROT)
    still = jnp.zeros(HEAD_DIM - ROT, F32)
    lanes = jnp.tile(jnp.concatenate([freqs, freqs, still]), LANES // HEAD_DIM)
    angles = places.astype(F32)[:, None] * lanes[None, :]
    return jnp.cos(angles), jnp.sin(angles)


def head_masks(rows):
    lane = lax.broadcasted_iota(jnp.int32, (rows, LANES), 1)
    return [lane // HEAD_DIM == h for h in range(LANES // HEAD_DIM)]


def causal(first, rows, keys):
    query = lax.broadcasted_iota(jnp.int32, (rows, keys), 0) + first
    key = lax.broadcasted_iota(jnp.int32, (rows, keys), 1)
    return key <= query


ROWS_COLS = ((1,), (1,))
COLS_COLS = ((0,), (0,))


def attend_kernel(
    q_in, k_in, v_in, bias, cosine, sine, out, q_out, k_out, v_out, stats
):
    length = q_in.shape[1]
    factor = float(HEAD_DIM) ** (-0.5)
    cos, sin = cosine[...], sine[...]
    q_out[0] = turn(q_in[0] + bias[0, 0:1], cos, sin).astype(BF16)
    k_out[0] = turn(k_in[0] + bias[0, 1:2], cos, sin).astype(BF16)
    v_out[0] = (v_in[0] + bias[0, 2:3]).astype(BF16)
    masks = head_masks(QBLOCK)
    for start in range(0, length, QBLOCK):
        end = start + QBLOCK
        query = q_out[0, start:end]
        key, value = k_out[0, 0:end], v_out[0, 0:end]
        keep = causal(start, QBLOCK, end)
        mixed, logs = None, None
        for mask in masks:
            logits = mm(jnp.where(mask, query, jnp.zeros_like(query)), key, ROWS_COLS) * factor
            logits = jnp.where(keep, logits, NEG)
            peak = jnp.max(logits, -1, keepdims=True)
            expo = jnp.exp(logits - peak)
            denom = jnp.sum(expo, -1, keepdims=True)
            part = mm((expo / denom).astype(BF16), value)
            log = jnp.broadcast_to(peak + jnp.log(denom), (QBLOCK, LANES))
            mixed = part if mixed is None else jnp.where(mask, part, mixed)
            logs = log if logs is None else jnp.where(mask, log, logs)
        out[0, start:end] = mixed.astype(BF16)
        stats[0, start:end] = logs


def attend_back_kernel(
    q_in, k_in, v_in, grad_in, stats, cosine, sine, dq_out, dk_out, dv_out, dk, dv
):
    length = q_in.shape[1]
    factor = float(HEAD_DIM) ** (-0.5)
    cos, sin = cosine[...], -sine[...]
    masks = head_masks(QBLOCK)
    dk[...] = jnp.zeros_like(dk)
    dv[...] = jnp.zeros_like(dv)
    for start in range(0, length, QBLOCK):
        end = start + QBLOCK
        query, grad = q_in[0, start:end], grad_in[0, start:end]
        key, value = k_in[0, 0:end], v_in[0, 0:end]
        keep = causal(start, QBLOCK, end)
        dq = None
        for number, mask in enumerate(masks):
            own_query = jnp.where(mask, query, jnp.zeros_like(query))
            own_grad = jnp.where(mask, grad, jnp.zeros_like(grad))
            log = stats[0, start:end, number * HEAD_DIM : number * HEAD_DIM + 1]
            logits = mm(own_query, key, ROWS_COLS) * factor
            probs = jnp.where(keep, jnp.exp(jnp.where(keep, logits, NEG) - log), 0.0)
            grad_probs = mm(own_grad, value, ROWS_COLS)
            inner = jnp.sum(grad_probs * probs, -1, keepdims=True)
            grad_logits = (probs * (grad_probs - inner)).astype(BF16)
            dv[0:end] += mm(probs.astype(BF16), own_grad, COLS_COLS)
            dk[0:end] += mm(grad_logits, own_query, COLS_COLS)
            part = mm(grad_logits, key)
            dq = part if dq is None else jnp.where(mask, part, dq)
        dq_out[0, start:end] = turn(dq * factor, cos[start:end], sin[start:end]).astype(BF16)
    dk_out[0] = turn(dk[...] * factor, cos, sin).astype(BF16)
    dv_out[0] = dv[...].astype(BF16)


def pair_spec(length):
    return pl.BlockSpec((1, length, LANES), lambda g: (0, 0, g))


def attend(parts, bias, tables):
    _, length, width = parts[0].shape
    spec = pair_spec(length)
    table = pl.BlockSpec((length, LANES), lambda g: (0, 0))
    shape = jax.ShapeDtypeStruct((1, length, width), BF16)
    return pl.pallas_call(
        attend_kernel,
        grid=(width // LANES,),
        in_specs=[spec] * 3
        + [pl.BlockSpec((1, 3, LANES), lambda g: (0, 0, g))]
        + [table] * 2,
        out_specs=[spec] * 5,
        out_shape=[shape] * 4 + [jax.ShapeDtypeStruct((1, length, width), F32)],
        name="attend",
    )(*parts, bias, *tables)


def attend_back(rotated, grad, stats, tables):
    _, length, width = grad.shape
    spec = pair_spec(length)
    table = pl.BlockSpec((length, LANES), lambda g: (0, 0))
    shape = jax.ShapeDtypeStruct((1, length, width), BF16)
    return pl.pallas_call(
        attend_back_kernel,
        grid=(width // LANES,),
        in_specs=[spec] * 5 + [table] * 2,
        out_specs=[spec] * 3,
        out_shape=[shape] * 3,
        scratch_shapes=[pltpu.VMEM((length, LANES), F32)] * 2,
        name="attend_back",
    )(*rotated, grad, stats, *tables)


def assemble_kernel(starts, *refs):
    pieces, left, right = refs[:-2], refs[-2], refs[-1]
    columns = left.shape[1]
    for number, piece in enumerate(pieces):
        rows = piece.shape[0]
        start = pl.multiple_of(starts[number], rows)
        left[pl.ds(start, rows), :] = piece[:, :columns].astype(F32)
        right[:, pl.ds(start, rows)] = piece[:, columns:].astype(F32).T


def assemble(pieces, columns):
    rows, total = pieces[0][1].shape
    length = rows * len(pieces)
    vmem = pl.BlockSpec(memory_space=pltpu.VMEM)
    return pl.pallas_call(
        assemble_kernel,
        in_specs=[pl.BlockSpec(memory_space=pltpu.SMEM)] + [vmem] * len(pieces),
        out_specs=[vmem, vmem],
        out_shape=[
            jax.ShapeDtypeStruct((length, columns), F32),
            jax.ShapeDtypeStruct((total - columns, length), F32),
        ],
        name="assemble",
    )(jnp.stack([start for start, _ in pieces]).astype(jnp.int32), *[piece for _, piece in pieces])


def body(
    hidden_in,
    positions,
    languages,
    ln1_gain,
    ln1_bias,
    w_qkv,
    b_qkv,
    w_out,
    ln2_gain,
    ln2_bias,
    w_gate,
    w_up,
    w_down,
    cotangent,
):
    tokens = hidden_in[0].astype(F32)
    count, width = tokens.shape
    size = lax.axis_size("seq")
    length = count * size
    unit = width // size
    language_ids = jnp.arange(LANGS, dtype=jnp.int32)
    marks_all = (languages[:, None] == language_ids[None, :]).astype(jnp.int32)
    language_totals = jnp.sum(marks_all, 0)
    own_language = lax.dynamic_slice_in_dim(languages, lax.axis_index("row"), 1, 0)
    own_marks = (own_language[0] == language_ids).astype(jnp.int32)
    own_count = jnp.sum(own_marks * language_totals)
    row_weight = F32(languages.shape[0] * length) / (LANGS * (own_count * length).astype(F32))
    gain_one, shift_one = ln1_gain.astype(F32), ln1_bias.astype(F32)
    gain_two, shift_two = ln2_gain.astype(F32), ln2_bias.astype(F32)

    normed_one, inverse_one = standardize(tokens)
    first_in = (normed_one * gain_one + shift_one).astype(BF16)
    bias_rows = jnp.broadcast_to(b_qkv[None], (BIAS_ROWS,) + b_qkv.shape)
    moved = to_heads(jnp.concatenate(own_chunks(w_qkv) + [bias_rows], 0))
    flows = len(flows_of())
    heads_b = jnp.concatenate([part[-1:] for part in moved], 0)[None].astype(F32)
    moved = jnp.concatenate([part[:-BIAS_ROWS] for part in moved], -1)
    heads_w = row_gather(jnp.split(moved, flows, 0))
    places = gather_places(positions[0])
    tables = rotary_tables(places)
    first_full = lax.all_gather(first_in, "seq", axis=0, tiled=True)
    projected = mm(first_full, heads_w)
    parts = [projected[None, :, i * unit : (i + 1) * unit] for i in range(3)]
    mixed, *rotated, stats = attend(parts, heads_b, tables)
    mixed = mixed[0]
    middle = tokens + scatter_tokens(
        lambda row: mm(rows_of(mixed, row, CORES * count), w_out), count
    )

    normed_two, inverse_two = standardize(middle)
    second_in = (normed_two * gain_two + shift_two).astype(BF16)
    grad_top = cotangent[0].astype(F32) * row_weight
    grad_top_full = lax.all_gather(grad_top.astype(BF16), "seq", axis=0, tiled=True)
    second_full = gather_tokens(second_in)
    gate = mm(second_full, w_gate)
    upward = mm(second_full, w_up)
    sigmoid_gate = jax.nn.sigmoid(gate)
    activated = gate * sigmoid_gate
    hidden = (activated * upward).astype(BF16)
    grad_hidden = mm(grad_top_full, w_down, ROWS_COLS)
    slope = sigmoid_gate * (1.0 + gate * (1.0 - sigmoid_gate))
    grad_gate = (grad_hidden * upward * slope).astype(BF16)
    grad_upward = (grad_hidden * activated).astype(BF16)
    feed_grads = (
        mm(second_full, grad_gate, COLS_COLS).astype(BF16),
        mm(second_full, grad_upward, COLS_COLS).astype(BF16),
        mm(hidden, grad_top_full, COLS_COLS).astype(BF16),
    )
    grad_second = scatter_tokens(
        lambda row: mm(rows_of(grad_gate, row, CORES * count), w_gate, ROWS_COLS)
        + mm(rows_of(grad_upward, row, CORES * count), w_up, ROWS_COLS),
        count,
        feed_grads,
    )
    feed_grads = lax.psum(feed_grads, "row")
    grad_middle = grad_top + norm_back(grad_second * gain_two, normed_two, inverse_two)
    grad_middle_full = gather_tokens(grad_middle.astype(BF16))
    feed_out = scatter_tokens(lambda row: mm(rows_of(hidden, row, CORES * count), w_down), count)
    grad_mixed = mm(grad_middle_full, w_out, ROWS_COLS).astype(BF16)
    grad_parts = attend_back(rotated, grad_mixed[None], stats, tables)
    grad_projected = jnp.concatenate([part[0] for part in grad_parts], 1)
    grad_b = jnp.sum(grad_projected.astype(F32), 0)
    grad_w_out = mm(grad_middle_full, mixed, COLS_COLS).astype(BF16)
    grad_w_qkv = mm(first_full, grad_projected, COLS_COLS).astype(BF16)
    attn_grads = jnp.concatenate([grad_w_qkv, grad_w_out], 1)
    attn_grads = jnp.concatenate(row_scatter(attn_grads), 0)
    back = from_heads([attn_grads[:, i * unit : (i + 1) * unit] for i in range(3)])
    attn_grads = jnp.concatenate([back, attn_grads[:, 3 * unit :]], 1)
    pieces = row_pieces(jnp.split(attn_grads, flows, 0))
    grad_w_qkv, grad_w_out = assemble(pieces, 3 * unit)
    grad_first = scatter_tokens(
        lambda row: mm(rows_of(grad_projected, row, CORES * count), heads_w, ROWS_COLS), count
    )
    output = (middle + feed_out).astype(BF16)[None]
    feed_grads = [part.astype(F32) for part in feed_grads]
    input_grad = (grad_middle + norm_back(grad_first * gain_one, normed_one, inverse_one)).astype(
        BF16
    )[None]

    def shards(vector):
        return vector.reshape(size, -1)

    own = jnp.arange(size, dtype=jnp.int32)[None, :, None] == lax.axis_index("seq")
    placed_b = jnp.where(own, grad_b.reshape(3, 1, unit), 0.0).reshape(size, 3 * unit)
    sums = small_sums(
        jnp.concatenate(
            [
                shards(jnp.sum(grad_first * normed_one, 0)),
                shards(jnp.sum(grad_first, 0)),
                shards(jnp.sum(grad_second * normed_two, 0)),
                shards(jnp.sum(grad_second, 0)),
                placed_b,
            ],
            1,
        )
    )
    return (
        output,
        input_grad,
        sums[:unit],
        sums[unit : 2 * unit],
        grad_w_qkv,
        sums[4 * unit :],
        grad_w_out,
        sums[2 * unit : 3 * unit],
        sums[3 * unit : 4 * unit],
        *feed_grads,
    )


def solution(mesh):
    placed = (
        P("row", "seq", None),
        P("row", "seq"),
        P(),
        P(),
        P(),
        P(None, "seq"),
        P("seq"),
        P("seq", None),
        P(),
        P(),
        P(None, "seq"),
        P(None, "seq"),
        P("seq", None),
        P("row", "seq", None),
    )
    return jax.shard_map(
        body,
        mesh=mesh,
        in_specs=placed,
        out_specs=(
            P("row", "seq", None),
            P("row", "seq", None),
            P("seq"),
            P("seq"),
            P(None, "seq"),
            P("seq"),
            P("seq", None),
            P("seq"),
            P("seq"),
            P(None, "seq"),
            P(None, "seq"),
            P("seq", None),
        ),
        check_vma=False,
    )
```

```python
import jax
import jax.numpy as jnp
from jax import lax
from jax.experimental import pallas as pl
from jax.experimental.pallas import tpu as pltpu
from jax.sharding import PartitionSpec as P


HEAD_DIM = 64
ROT = 16
LANGS = 7
CORES = 2
LANES = 128
QBLOCK = 256
SPLITS = 2
BIAS_ROWS = 16

EPS = 1e-05
NEG = -1e30
BASE = 10000.0

F32 = jnp.float32
BF16 = jnp.bfloat16


def standardize(values):
    center = values - jnp.mean(values, -1, keepdims=True)
    spread = jnp.mean(center * center, -1, keepdims=True)
    inverse = lax.rsqrt(spread + EPS)
    return (center * inverse, inverse)


def norm_back(grad_normed, normed, inverse):
    return inverse * (
        grad_normed
        - jnp.mean(grad_normed, -1, keepdims=True)
        - normed * jnp.mean(grad_normed * normed, -1, keepdims=True)
    )


def mm(left, right, dims=((1,), (0,))):
    return lax.dot_general(left, right, (dims, ((), ())), preferred_element_type=F32)


def pick(array, at, axis=0):
    return lax.dynamic_index_in_dim(array, at, axis, keepdims=False)


def rows_of(array, start, size):
    return lax.dynamic_slice_in_dim(array, start, size, 0)


def swap_cores(value):
    size = lax.axis_size("seq")
    return lax.ppermute(value, "seq", [(d, d ^ 1) for d in range(size)])


def ring(value):
    size = lax.axis_size("seq")
    to = [(d, (d + CORES) % size) for d in range(size)]
    return [lax.ppermute(part, "seq", to) for part in value]


def cut(value):
    rows = value.shape[0] // SPLITS
    return [value[k * rows : (k + 1) * rows] for k in range(SPLITS)]


def gather_places(local):
    size = lax.axis_size("seq")
    me = lax.axis_index("seq")
    have, bit = local, 1
    while bit < size:
        other = lax.ppermute(have, "seq", [(d, d ^ bit) for d in range(size)])
        own = (me // bit) % 2
        have = jnp.where(
            own == 0, jnp.concatenate([have, other]), jnp.concatenate([other, have])
        )
        bit *= 2
    return have


def gather_tokens(local):
    size = lax.axis_size("seq")
    me = lax.axis_index("seq")
    chips = size // CORES
    chip, core = me // CORES, me % CORES
    count = local.shape[0]
    full = jnp.zeros((size * count,) + local.shape[1:], local.dtype)
    piece = cut(local)
    for step in range(chips):
        following = None
        if step + 1 < chips:
            following = ring(piece)
        base = ((chip - step) % chips) * CORES
        rows = count // SPLITS
        for k, part in enumerate(piece):
            other = swap_cores(part)
            full = lax.dynamic_update_slice_in_dim(full, part, (base + core) * count + k * rows, 0)
            full = lax.dynamic_update_slice_in_dim(
                full, other, (base + 1 - core) * count + k * rows, 0
            )
        piece = following
    return full


def scatter_tokens(block_of, count):
    size = lax.axis_size("seq")
    me = lax.axis_index("seq")
    chips = size // CORES
    chip, core = me // CORES, me % CORES
    rows = count // SPLITS
    carried = [None] * SPLITS
    for step in range(1, chips + 1):
        row = ((chip - step) % chips) * CORES * count
        block = block_of(row)
        totals = []
        for k in range(SPLITS):
            other = swap_cores(rows_of(block, (1 - core) * count + k * rows, rows).astype(BF16))
            total = rows_of(block, core * count + k * rows, rows) + other.astype(F32)
            if carried[k] is not None:
                total = total + carried[k].astype(F32)
            totals.append(total)
        if step < chips:
            carried = ring([total.astype(BF16) for total in totals])
    return jnp.concatenate(totals, 0)


def row_bits():
    size = lax.axis_size("row")
    return [1 << b for b in range(size.bit_length() - 1)]


def row_swap(value, bit):
    size = lax.axis_size("row")
    return lax.ppermute(value, "row", [(d, d ^ bit) for d in range(size)])


def side(bit):
    return (lax.axis_index("row") // bit) % 2


def flows_of():
    bits = row_bits()
    return [bits, bits[1:] + bits[:1]] if len(bits) > 1 else [bits]


def place_in(order):
    place = 0
    for bit in order:
        place = place * 2 + side(bit)
    return place


def row_scatter(value):
    flows = flows_of()
    done = []
    for number, order in enumerate(flows):
        rows = value.shape[0] // len(flows)
        part = value[number * rows : (number + 1) * rows]
        for bit in order:
            half = part.shape[0] // 2
            sent = row_swap(rows_of(part, (1 - side(bit)) * half, half), bit)
            kept = rows_of(part, side(bit) * half, half)
            part = (kept.astype(F32) + sent.astype(F32)).astype(value.dtype)
        done.append(part)
    return done


def row_pieces(chunks):
    rows = chunks[0].shape[0]
    total = rows * lax.axis_size("row")
    found = []
    for number, order in enumerate(flows_of()):
        pieces = [(place_in(order), chunks[number])]
        for level, bit in enumerate(reversed(order)):
            flip = (1 - 2 * side(bit)) << level
            pieces = pieces + [(at + flip, row_swap(piece, bit)) for at, piece in pieces]
        found += [(number * total + at * rows, piece) for at, piece in pieces]
    return found


def row_gather(chunks):
    pieces = row_pieces(chunks)
    full = jnp.zeros((chunks[0].shape[0] * len(pieces), chunks[0].shape[1]), chunks[0].dtype)
    for start, piece in pieces:
        full = lax.dynamic_update_slice_in_dim(full, piece, start, 0)
    return full


def own_chunks(value):
    flows = flows_of()
    total = value.shape[0] // len(flows)
    rows = total // lax.axis_size("row")
    return [
        rows_of(value, number * total + place_in(order) * rows, rows)
        for number, order in enumerate(flows)
    ]


def to_heads(units):
    size = lax.axis_size("seq")
    me = lax.axis_index("seq")
    unit = units.shape[-1] // 3
    got = jnp.stack(
        [
            lax.ppermute(
                units[..., i * unit : (i + 1) * unit],
                "seq",
                [(d, (3 * d + i) % size) for d in range(size)],
            )
            for i in range(3)
        ]
    )
    return [pick(got, (me + part * size) % 3) for part in range(3)]


def from_heads(parts):
    size = lax.axis_size("seq")
    me = lax.axis_index("seq")
    stacked = jnp.stack(parts)
    back = []
    for i in range(3):
        part = ((i - me) * pow(size, -1, 3)) % 3
        back.append(
            lax.ppermute(
                pick(stacked, part), "seq", [((3 * d + i) % size, d) for d in range(size)]
            )
        )
    return jnp.concatenate(back, -1)


def small_sums(values):
    size = lax.axis_size("seq")
    me = lax.axis_index("seq")
    part = values
    bit = size // 2
    while bit:
        own = (me // bit) % 2
        halves = part.reshape((2, part.shape[0] // 2) + part.shape[1:])
        part = pick(halves, own) + lax.ppermute(
            pick(halves, 1 - own), "seq", [(d, d ^ bit) for d in range(size)]
        )
        bit //= 2
    part = part[0]
    for bit in row_bits():
        part = part + row_swap(part, bit)
    return part


def turn(value, cosine, sine):
    lane = lax.broadcasted_iota(jnp.int32, sine.shape, 1) % HEAD_DIM
    half = ROT // 2
    low = jnp.where(lane < half, -sine, 0.0)
    high = jnp.where(lane < half, 0.0, sine)
    return (
        value * cosine
        + pltpu.roll(value, LANES - half, 1) * low
        + pltpu.roll(value, half, 1) * high
    )


def rotary_tables(places):
    half = ROT // 2
    freqs = BASE ** (-(jnp.arange(half, dtype=F32) * 2.0) / ROT)
    still = jnp.zeros(HEAD_DIM - ROT, F32)
    lanes = jnp.tile(jnp.concatenate([freqs, freqs, still]), LANES // HEAD_DIM)
    angles = places.astype(F32)[:, None] * lanes[None, :]
    return jnp.cos(angles), jnp.sin(angles)


def head_masks(rows):
    lane = lax.broadcasted_iota(jnp.int32, (rows, LANES), 1)
    return [lane // HEAD_DIM == h for h in range(LANES // HEAD_DIM)]


def causal(first, rows, keys):
    query = lax.broadcasted_iota(jnp.int32, (rows, keys), 0) + first
    key = lax.broadcasted_iota(jnp.int32, (rows, keys), 1)
    return key <= query


ROWS_COLS = ((1,), (1,))
COLS_COLS = ((0,), (0,))


def attend_kernel(
    q_in, k_in, v_in, bias, cosine, sine, out, q_out, k_out, v_out, stats
):
    length = q_in.shape[1]
    factor = float(HEAD_DIM) ** (-0.5)
    cos, sin = cosine[...], sine[...]
    q_out[0] = turn(q_in[0] + bias[0, 0:1], cos, sin).astype(BF16)
    k_out[0] = turn(k_in[0] + bias[0, 1:2], cos, sin).astype(BF16)
    v_out[0] = (v_in[0] + bias[0, 2:3]).astype(BF16)
    masks = head_masks(QBLOCK)
    for start in range(0, length, QBLOCK):
        end = start + QBLOCK
        query = q_out[0, start:end]
        key, value = k_out[0, 0:end], v_out[0, 0:end]
        keep = causal(start, QBLOCK, end)
        mixed, logs = None, None
        for mask in masks:
            logits = mm(jnp.where(mask, query, jnp.zeros_like(query)), key, ROWS_COLS) * factor
            logits = jnp.where(keep, logits, NEG)
            peak = jnp.max(logits, -1, keepdims=True)
            expo = jnp.exp(logits - peak)
            denom = jnp.sum(expo, -1, keepdims=True)
            part = mm((expo / denom).astype(BF16), value)
            log = jnp.broadcast_to(peak + jnp.log(denom), (QBLOCK, LANES))
            mixed = part if mixed is None else jnp.where(mask, part, mixed)
            logs = log if logs is None else jnp.where(mask, log, logs)
        out[0, start:end] = mixed.astype(BF16)
        stats[0, start:end] = logs


def attend_back_kernel(
    q_in, k_in, v_in, grad_in, stats, cosine, sine, dq_out, dk_out, dv_out, dk, dv
):
    length = q_in.shape[1]
    factor = float(HEAD_DIM) ** (-0.5)
    cos, sin = cosine[...], -sine[...]
    masks = head_masks(QBLOCK)
    dk[...] = jnp.zeros_like(dk)
    dv[...] = jnp.zeros_like(dv)
    for start in range(0, length, QBLOCK):
        end = start + QBLOCK
        query, grad = q_in[0, start:end], grad_in[0, start:end]
        key, value = k_in[0, 0:end], v_in[0, 0:end]
        keep = causal(start, QBLOCK, end)
        dq = None
        for number, mask in enumerate(masks):
            own_query = jnp.where(mask, query, jnp.zeros_like(query))
            own_grad = jnp.where(mask, grad, jnp.zeros_like(grad))
            log = stats[0, start:end, number * HEAD_DIM : number * HEAD_DIM + 1]
            logits = mm(own_query, key, ROWS_COLS) * factor
            probs = jnp.where(keep, jnp.exp(jnp.where(keep, logits, NEG) - log), 0.0)
            grad_probs = mm(own_grad, value, ROWS_COLS)
            inner = jnp.sum(grad_probs * probs, -1, keepdims=True)
            grad_logits = (probs * (grad_probs - inner)).astype(BF16)
            dv[0:end] += mm(probs.astype(BF16), own_grad, COLS_COLS)
            dk[0:end] += mm(grad_logits, own_query, COLS_COLS)
            part = mm(grad_logits, key)
            dq = part if dq is None else jnp.where(mask, part, dq)
        dq_out[0, start:end] = turn(dq * factor, cos[start:end], sin[start:end]).astype(BF16)
    dk_out[0] = turn(dk[...] * factor, cos, sin).astype(BF16)
    dv_out[0] = dv[...].astype(BF16)


def pair_spec(length):
    return pl.BlockSpec((1, length, LANES), lambda g: (0, 0, g))


def attend(parts, bias, tables):
    _, length, width = parts[0].shape
    spec = pair_spec(length)
    table = pl.BlockSpec((length, LANES), lambda g: (0, 0))
    shape = jax.ShapeDtypeStruct((1, length, width), BF16)
    return pl.pallas_call(
        attend_kernel,
        grid=(width // LANES,),
        in_specs=[spec] * 3
        + [pl.BlockSpec((1, 3, LANES), lambda g: (0, 0, g))]
        + [table] * 2,
        out_specs=[spec] * 5,
        out_shape=[shape] * 4 + [jax.ShapeDtypeStruct((1, length, width), F32)],
        name="attend",
    )(*parts, bias, *tables)


def attend_back(rotated, grad, stats, tables):
    _, length, width = grad.shape
    spec = pair_spec(length)
    table = pl.BlockSpec((length, LANES), lambda g: (0, 0))
    shape = jax.ShapeDtypeStruct((1, length, width), BF16)
    return pl.pallas_call(
        attend_back_kernel,
        grid=(width // LANES,),
        in_specs=[spec] * 5 + [table] * 2,
        out_specs=[spec] * 3,
        out_shape=[shape] * 3,
        scratch_shapes=[pltpu.VMEM((length, LANES), F32)] * 2,
        name="attend_back",
    )(*rotated, grad, stats, *tables)


def assemble_kernel(starts, *refs):
    pieces, left, right = refs[:-2], refs[-2], refs[-1]
    columns = left.shape[1]
    for number, piece in enumerate(pieces):
        rows = piece.shape[0]
        start = pl.multiple_of(starts[number], rows)
        left[pl.ds(start, rows), :] = piece[:, :columns].astype(F32)
        right[:, pl.ds(start, rows)] = piece[:, columns:].astype(F32).T


def assemble(pieces, columns):
    rows, total = pieces[0][1].shape
    length = rows * len(pieces)
    vmem = pl.BlockSpec(memory_space=pltpu.VMEM)
    return pl.pallas_call(
        assemble_kernel,
        in_specs=[pl.BlockSpec(memory_space=pltpu.SMEM)] + [vmem] * len(pieces),
        out_specs=[vmem, vmem],
        out_shape=[
            jax.ShapeDtypeStruct((length, columns), F32),
            jax.ShapeDtypeStruct((total - columns, length), F32),
        ],
        name="assemble",
    )(jnp.stack([start for start, _ in pieces]).astype(jnp.int32), *[piece for _, piece in pieces])


def body(
    hidden_in,
    positions,
    languages,
    ln1_gain,
    ln1_bias,
    w_qkv,
    b_qkv,
    w_out,
    ln2_gain,
    ln2_bias,
    w_gate,
    w_up,
    w_down,
    cotangent,
):
    tokens = hidden_in[0].astype(F32)
    count, width = tokens.shape
    size = lax.axis_size("seq")
    length = count * size
    unit = width // size
    language_ids = jnp.arange(LANGS, dtype=jnp.int32)
    marks_all = (languages[:, None] == language_ids[None, :]).astype(jnp.int32)
    language_totals = jnp.sum(marks_all, 0)
    own_language = lax.dynamic_slice_in_dim(languages, lax.axis_index("row"), 1, 0)
    own_marks = (own_language[0] == language_ids).astype(jnp.int32)
    own_count = jnp.sum(own_marks * language_totals)
    row_weight = F32(languages.shape[0] * length) / (LANGS * (own_count * length).astype(F32))
    gain_one, shift_one = ln1_gain.astype(F32), ln1_bias.astype(F32)
    gain_two, shift_two = ln2_gain.astype(F32), ln2_bias.astype(F32)

    normed_one, inverse_one = standardize(tokens)
    first_in = (normed_one * gain_one + shift_one).astype(BF16)
    bias_rows = jnp.broadcast_to(b_qkv[None], (BIAS_ROWS,) + b_qkv.shape)
    moved = to_heads(jnp.concatenate(own_chunks(w_qkv) + [bias_rows], 0))
    flows = len(flows_of())
    heads_b = jnp.concatenate([part[-1:] for part in moved], 0)[None].astype(F32)
    moved = jnp.concatenate([part[:-BIAS_ROWS] for part in moved], -1)
    heads_w = row_gather(jnp.split(moved, flows, 0))
    places = gather_places(positions[0])
    tables = rotary_tables(places)
    first_full = lax.all_gather(first_in, "seq", axis=0, tiled=True)
    projected = mm(first_full, heads_w)
    parts = [projected[None, :, i * unit : (i + 1) * unit] for i in range(3)]
    mixed, *rotated, stats = attend(parts, heads_b, tables)
    mixed = mixed[0]
    middle = tokens + scatter_tokens(
        lambda row: mm(rows_of(mixed, row, CORES * count), w_out), count
    )

    normed_two, inverse_two = standardize(middle)
    second_in = (normed_two * gain_two + shift_two).astype(BF16)
    grad_top = cotangent[0].astype(F32) * row_weight
    grad_top_full = lax.all_gather(grad_top.astype(BF16), "seq", axis=0, tiled=True)
    second_full = gather_tokens(second_in)
    gate = mm(second_full, w_gate)
    upward = mm(second_full, w_up)
    sigmoid_gate = jax.nn.sigmoid(gate)
    activated = gate * sigmoid_gate
    hidden = (activated * upward).astype(BF16)
    grad_hidden = mm(grad_top_full, w_down, ROWS_COLS)
    slope = sigmoid_gate * (1.0 + gate * (1.0 - sigmoid_gate))
    grad_gate = (grad_hidden * upward * slope).astype(BF16)
    grad_upward = (grad_hidden * activated).astype(BF16)
    feed_grads = (
        mm(second_full, grad_gate, COLS_COLS).astype(BF16),
        mm(second_full, grad_upward, COLS_COLS).astype(BF16),
        mm(hidden, grad_top_full, COLS_COLS).astype(BF16),
    )
    grad_second = scatter_tokens(
        lambda row: mm(rows_of(grad_gate, row, CORES * count), w_gate, ROWS_COLS)
        + mm(rows_of(grad_upward, row, CORES * count), w_up, ROWS_COLS),
        count,
    )
    feed_grads = lax.psum(feed_grads, "row")
    grad_middle = grad_top + norm_back(grad_second * gain_two, normed_two, inverse_two)
    grad_middle_full = gather_tokens(grad_middle.astype(BF16))
    feed_out = scatter_tokens(lambda row: mm(rows_of(hidden, row, CORES * count), w_down), count)
    grad_mixed = mm(grad_middle_full, w_out, ROWS_COLS).astype(BF16)
    grad_parts = attend_back(rotated, grad_mixed[None], stats, tables)
    grad_projected = jnp.concatenate([part[0] for part in grad_parts], 1)
    grad_b = jnp.sum(grad_projected.astype(F32), 0)
    grad_w_out = mm(grad_middle_full, mixed, COLS_COLS).astype(BF16)
    grad_w_qkv = mm(first_full, grad_projected, COLS_COLS).astype(BF16)
    attn_grads = jnp.concatenate([grad_w_qkv, grad_w_out], 1)
    attn_grads = jnp.concatenate(row_scatter(attn_grads), 0)
    back = from_heads([attn_grads[:, i * unit : (i + 1) * unit] for i in range(3)])
    attn_grads = jnp.concatenate([back, attn_grads[:, 3 * unit :]], 1)
    pieces = row_pieces(jnp.split(attn_grads, flows, 0))
    grad_w_qkv, grad_w_out = assemble(pieces, 3 * unit)
    grad_first = scatter_tokens(
        lambda row: mm(rows_of(grad_projected, row, CORES * count), heads_w, ROWS_COLS), count
    )
    output = (middle + feed_out).astype(BF16)[None]
    feed_grads = [part.astype(F32) for part in feed_grads]
    input_grad = (grad_middle + norm_back(grad_first * gain_one, normed_one, inverse_one)).astype(
        BF16
    )[None]

    def shards(vector):
        return vector.reshape(size, -1)

    own = jnp.arange(size, dtype=jnp.int32)[None, :, None] == lax.axis_index("seq")
    placed_b = jnp.where(own, grad_b.reshape(3, 1, unit), 0.0).reshape(size, 3 * unit)
    sums = small_sums(
        jnp.concatenate(
            [
                shards(jnp.sum(grad_first * normed_one, 0)),
                shards(jnp.sum(grad_first, 0)),
                shards(jnp.sum(grad_second * normed_two, 0)),
                shards(jnp.sum(grad_second, 0)),
                placed_b,
            ],
            1,
        )
    )
    return (
        output,
        input_grad,
        sums[:unit],
        sums[unit : 2 * unit],
        grad_w_qkv,
        sums[4 * unit :],
        grad_w_out,
        sums[2 * unit : 3 * unit],
        sums[3 * unit : 4 * unit],
        *feed_grads,
    )


def solution(mesh):
    placed = (
        P("row", "seq", None),
        P("row", "seq"),
        P(),
        P(),
        P(),
        P(None, "seq"),
        P("seq"),
        P("seq", None),
        P(),
        P(),
        P(None, "seq"),
        P(None, "seq"),
        P("seq", None),
        P("row", "seq", None),
    )
    return jax.shard_map(
        body,
        mesh=mesh,
        in_specs=placed,
        out_specs=(
            P("row", "seq", None),
            P("row", "seq", None),
            P("seq"),
            P("seq"),
            P(None, "seq"),
            P("seq"),
            P("seq", None),
            P("seq"),
            P("seq"),
            P(None, "seq"),
            P(None, "seq"),
            P("seq", None),
        ),
        check_vma=False,
    )
```
